32 devices in a mesh: section: 4 (over y, x), tp: 8 (over z, core).
Axes of the slice: x: 2, y: 2, z: 4, core: 2. Of those that a mesh axis runs over, the one named last changes fastest.
Arguments:
- inputs_now: bfloat16 [1536, 6144], P(('section', 'tp')), may hold values from -6 to 6
- cotangents: bfloat16 [1536, 6144], P(('section', 'tp')), may hold values from -6 to 6
- stashed: bfloat16 [3, 1536, 6144], P(None, ('section', 'tp')), may hold values from -6 to 6
- plan: int32 [4], replicated, may hold values from 0 to 2
- fwd_scores: bfloat16 [4, 48, 384, 384], P('section', 'tp'), may hold values from -9 to 300, as said below
- back_scores: bfloat16 [4, 48, 384, 384], P('section', 'tp'), may hold values from -9 to 300, as said below
- value_weight: bfloat16 [4, 6144, 6144], P('section', None, 'tp'), may hold values from -0.078125 to 0.078125
- out_weight: bfloat16 [4, 6144, 6144], P('section', 'tp'), may hold values from -0.21875 to 0.21875
Outputs:
- handed_on: bfloat16 [1536, 6144], P(('section', 'tp'))
- grad_back: bfloat16 [1536, 6144], P(('section', 'tp'))
- stash_next: bfloat16 [3, 1536, 6144], P(None, ('section', 'tp'))
- value_grad: bfloat16 [4, 6144, 6144], P('section', None, 'tp')
- out_grad: bfloat16 [4, 6144, 6144], P('section', 'tp')
The draws below stay inside these ranges and needn't reach their ends.
Inputs may be any that keep to these rules, and one draw needn't show every extreme that they name: plan[s] names the slot, in the stash rows of section 3 - s, that holds section s's micro-batch for this tick's backward. `fwd_scores`: logits of keys later than the query are never read. `back_scores`: logits of keys later than the query are never read.
All inputs are finite; a program needn't handle non-finite values.
Results may differ from the reference program's by a relative error of at most 0.012.
Values may be sent and summed in bfloat16 or wider, within the bound.
A program may use at most 192 MiB of HBM per device.

```python
import jax
import jax.numpy as jnp
from jax import lax

D = 6144
HEADS = 48
HEAD = 128
TOK = 384
K = 3
HW = 6144
ALL_TOK = 1536
N_SECTION = 4
N_TP = 8


def score_draw(key):
    shape = (N_SECTION, HEADS, TOK, TOK)
    return jnp.clip(2.0 * jax.random.normal(jax.random.fold_in(key, 13), shape, jnp.float32), -9.0, 9.0)


def draw_fwd_scores(key, part):
    return score_draw(jax.random.fold_in(key, 101)).astype(jnp.bfloat16)


def draw_back_scores(key, part):
    return score_draw(jax.random.fold_in(key, 202)).astype(jnp.bfloat16)


def set_ends(drawn, rng, least, top_value):
    shape = drawn.shape
    spot = [jax.random.randint(jax.random.fold_in(rng, axis), (), 0, shape[axis]) for axis in range(len(shape))]
    drawn = drawn.at[tuple(spot)].set(least)
    longest = shape.index(max(shape))
    spot[longest] = (spot[longest] + 1) % shape[longest]
    return drawn.at[tuple(spot)].set(top_value)


def steps_of(own_key, extent, shards, least, high):
    def one(position, parts):
        heights = jax.random.uniform(jax.random.fold_in(jax.random.fold_in(own_key, 6), position), (parts,), jnp.float32, least / len(shards), high / len(shards))
        return jnp.repeat(jnp.exp(heights), extent[position] // parts).reshape((-1,) + (1,) * (len(extent) - position - 1))

    loudness = one(*shards[0])
    for cut in shards[1:]:
        loudness = loudness * one(*cut)
    return loudness


def noise(rng, shape, deviation, reach, pieces=(), kind=jnp.bfloat16):
    entries = deviation * jax.random.normal(rng, shape, jnp.float32)
    if pieces:
        entries = entries * steps_of(rng, shape, pieces, -0.22, 0.18)
    return jnp.clip(entries, -reach, reach).astype(kind)


def setup_inputs(seed: int = 0) -> dict:
    splits = jax.random.split(jax.random.key(seed), 9)
    return {
        "inputs_now": noise(splits[0], (ALL_TOK, D), 1.0, 6.0, ((0, 32),)),
        "cotangents": noise(splits[1], (ALL_TOK, D), 1.0, 6.0, ((0, 32),)),
        "stashed": noise(splits[2], (K, ALL_TOK, D), 1.0, 6.0, ((1, 32),)),
        "plan": set_ends(jax.random.randint(splits[3], (N_SECTION,), 0, K), jax.random.fold_in(splits[3], 1), 0, K - 1).astype(jnp.int32),
        "fwd_scores": draw_fwd_scores(jax.random.fold_in(splits[8], 71), 0),
        "back_scores": draw_back_scores(jax.random.fold_in(splits[8], 71), 0),
        "value_weight": noise(splits[6], (N_SECTION, D, HW), D ** -0.5, 0.078125, ((0, 4), (2, 8))),
        "out_weight": noise(splits[7], (N_SECTION, HW, D), (HW // 8) ** -0.5, 0.21875, ((0, 4), (1, 8))),
    }


eps = 1e-05

def normalize(layer_rows):
    average = lax.optimization_barrier(jnp.mean(layer_rows, axis=-1, keepdims=True))
    centred = layer_rows - average
    inv_scale = lax.rsqrt(lax.optimization_barrier(jnp.mean(centred * centred, axis=-1, keepdims=True)) + eps)
    return (centred * inv_scale, inv_scale)

def causal_softmax(scores):
    logits = scores.astype(jnp.float32)
    rows = logits.shape[-1]
    causal = jnp.arange(rows)[:, None] >= jnp.arange(rows)[None, :]
    logits = jnp.where(causal, logits, -1e+30)
    row_top = lax.optimization_barrier(jnp.max(logits, axis=-1, keepdims=True))
    raised = jnp.where(causal, jnp.exp(logits - row_top), 0.0)
    return (raised / lax.optimization_barrier(jnp.sum(raised, axis=-1, keepdims=True))).astype(jnp.bfloat16)

def mix_heads(weights, value_rows):
    by_head = value_rows.reshape(TOK, HEADS, HEAD).astype(jnp.float32)
    mixed = jnp.einsum('hqk,khe->qhe', weights.astype(jnp.float32), by_head)
    return mixed.reshape(TOK, HW).astype(jnp.bfloat16)

def rounded(value):
    return lax.optimization_barrier(value.astype(jnp.bfloat16)).astype(jnp.float32)

def reference(inputs_now, cotangents, stashed, plan, fwd_scores, back_scores, value_weight, out_weight):
    col_share = HW // N_TP
    forward_outs = []
    backward_outs = []
    grads_value = []
    grads_out = []
    stash_blocks = []
    for section_idx in range(N_SECTION):
        mirror = N_SECTION - 1 - section_idx
        weight_in = value_weight[section_idx]
        weight_out = out_weight[section_idx]
        layer_rows = inputs_now[section_idx * TOK:(section_idx + 1) * TOK].astype(jnp.float32)
        unit_rows, _ = normalize(layer_rows)
        normed = unit_rows.astype(jnp.bfloat16)
        values = jnp.dot(normed, weight_in, preferred_element_type=jnp.float32).astype(jnp.bfloat16)
        context = mix_heads(causal_softmax(fwd_scores[section_idx]), values)
        partial_value = jnp.einsum('tph,phd->ptd', context.reshape(TOK, N_TP, col_share).astype(jnp.float32), weight_out.reshape(N_TP, col_share, D).astype(jnp.float32))
        branch = lax.optimization_barrier(jnp.sum(rounded(partial_value), axis=0))
        forward_outs.append((layer_rows + branch).astype(jnp.bfloat16))
        slot_index = plan[section_idx].astype(jnp.int32)
        held = lax.dynamic_index_in_dim(stashed, slot_index, 0, keepdims=False)
        stash_rows = held[mirror * TOK:(mirror + 1) * TOK].astype(jnp.float32)
        stash_unit, stash_scale = normalize(stash_rows)
        stash_normed = stash_unit.astype(jnp.bfloat16)
        stash_values = jnp.dot(stash_normed, weight_in, preferred_element_type=jnp.float32).astype(jnp.bfloat16)
        back_probs = causal_softmax(back_scores[section_idx])
        stash_context = mix_heads(back_probs, stash_values)
        upstream = cotangents[section_idx * TOK:(section_idx + 1) * TOK]
        grads_out.append(jnp.dot(stash_context.T, upstream, preferred_element_type=jnp.float32).astype(jnp.bfloat16))
        context_grad = jnp.dot(upstream, weight_out.T, preferred_element_type=jnp.float32).astype(jnp.bfloat16)
        value_back = jnp.einsum('hqk,qhe->khe', back_probs.astype(jnp.float32), context_grad.reshape(TOK, HEADS, HEAD).astype(jnp.float32)).reshape(TOK, HW).astype(jnp.bfloat16)
        grads_value.append(jnp.dot(stash_normed.T, value_back, preferred_element_type=jnp.float32).astype(jnp.bfloat16))
        partial_back = jnp.einsum('tph,dph->ptd', value_back.reshape(TOK, N_TP, col_share).astype(jnp.float32), weight_in.reshape(D, N_TP, col_share).astype(jnp.float32))
        norm_grad = lax.optimization_barrier(jnp.sum(rounded(partial_back), axis=0))
        input_grad = upstream.astype(jnp.float32) + stash_scale * (norm_grad - lax.optimization_barrier(jnp.mean(norm_grad, axis=-1, keepdims=True)) - stash_unit * lax.optimization_barrier(jnp.mean(norm_grad * stash_unit, axis=-1, keepdims=True)))
        backward_outs.append(input_grad.astype(jnp.bfloat16))
        stash_block = stashed[:, section_idx * TOK:(section_idx + 1) * TOK]
        incoming = inputs_now[mirror * TOK:(mirror + 1) * TOK]
        stash_block = lax.dynamic_update_index_in_dim(stash_block, incoming, plan[mirror].astype(jnp.int32), 0)
        stash_blocks.append(stash_block)
    handed_on = jnp.concatenate([forward_outs[(block - 1) % N_SECTION] for block in range(N_SECTION)], axis=0)
    grad_back = jnp.concatenate([backward_outs[(block + 1) % N_SECTION] for block in range(N_SECTION)], axis=0)
    stash_next = jnp.concatenate(stash_blocks, axis=1)
    return (handed_on, grad_back, stash_next, jnp.stack(grads_value), jnp.stack(grads_out))
```

```python
import jax
import jax.numpy as jnp
from jax import lax
from jax.sharding import PartitionSpec as P


HEAD = 128


eps = 1e-05


def passed_along(array, axis, by):
    size = lax.axis_size(axis)
    return lax.ppermute(array, axis, [(i, (i + by) % size) for i in range(size)])


def normalize(layer_rows):
    average = jnp.mean(layer_rows, axis=-1, keepdims=True)
    centred = layer_rows - average
    inv_scale = lax.rsqrt(jnp.mean(centred * centred, axis=-1, keepdims=True) + eps)
    return (centred * inv_scale, inv_scale)


def causal_softmax(scores):
    logits = scores.astype(jnp.float32)
    rows = logits.shape[-1]
    causal = lax.broadcasted_iota(jnp.int32, (rows, rows), 0) >= lax.broadcasted_iota(
        jnp.int32, (rows, rows), 1
    )
    logits = jnp.where(causal, logits, -1e30)
    row_top = jnp.max(logits, axis=-1, keepdims=True)
    raised = jnp.where(causal, jnp.exp(logits - row_top), 0.0)
    return (raised / jnp.sum(raised, axis=-1, keepdims=True)).astype(jnp.bfloat16)


def mix_heads(weights, value_rows):
    rows = value_rows.shape[0]
    head_count = weights.shape[0]
    by_head = value_rows.reshape(rows, head_count, HEAD)
    mixed = jnp.einsum("hqk,khe->qhe", weights, by_head, preferred_element_type=jnp.float32)
    return mixed.reshape(rows, head_count * HEAD).astype(jnp.bfloat16)


def reduce_rows(partial):
    return lax.psum_scatter(
        partial.astype(jnp.bfloat16), "tp", scatter_dimension=0, tiled=True
    ).astype(jnp.float32)


def mirrored(array):
    size = lax.axis_size("section")
    return lax.ppermute(array, "section", [(i, size - 1 - i) for i in range(size)])


def per_device(
    inputs_now, cotangents, stashed, plan, fwd_scores, back_scores, value_weight, out_weight
):
    tp_count = lax.axis_size("tp")
    sections = lax.axis_size("section")
    section_idx = lax.axis_index("section")
    mirror = sections - 1 - section_idx
    share_rows = inputs_now.shape[0]
    all_rows = share_rows * tp_count
    weight_in = value_weight[0]
    weight_out = out_weight[0]
    col_share = weight_in.shape[1]
    head_count = back_scores.shape[1]

    rows_cot = lax.all_gather(cotangents, "tp", axis=0, tiled=True)
    lookup = jnp.arange(sections, dtype=jnp.int32)
    owner_slot = jnp.sum(jnp.where(lookup == mirror, plan, 0))
    guest_rows = lax.dynamic_index_in_dim(stashed, owner_slot, 0, keepdims=False)
    stored = mirrored(guest_rows)
    arrived = mirrored(inputs_now)
    layer_rows = inputs_now.astype(jnp.float32)
    unit_rows, _ = normalize(layer_rows)
    normed = unit_rows.astype(jnp.bfloat16)
    rows_now = lax.all_gather(normed, "tp", axis=0, tiled=True)

    back_probs = causal_softmax(back_scores[0])
    fwd_probs = causal_softmax(fwd_scores[0])

    rows_grad = jnp.einsum(
        "td,hd->th", rows_cot, weight_out, preferred_element_type=jnp.float32
    ).astype(jnp.bfloat16)
    value_back = (
        jnp.einsum(
            "hqk,qhe->khe",
            back_probs,
            rows_grad.reshape(all_rows, head_count, HEAD),
            preferred_element_type=jnp.float32,
        )
        .reshape(all_rows, col_share)
        .astype(jnp.bfloat16)
    )
    partial_back = jnp.einsum(
        "th,dh->td", value_back, weight_in, preferred_element_type=jnp.float32
    )
    norm_grad = reduce_rows(partial_back)

    stash_unit, stash_scale = normalize(stored.astype(jnp.float32))
    stash_normed = stash_unit.astype(jnp.bfloat16)
    rows_norm = lax.all_gather(stash_normed, "tp", axis=0, tiled=True)

    rows_now, stash_normed = lax.optimization_barrier((rows_now, stash_normed))
    values = jnp.dot(rows_now, weight_in, preferred_element_type=jnp.float32).astype(jnp.bfloat16)
    context = mix_heads(fwd_probs, values)
    partial = jnp.dot(context, weight_out, preferred_element_type=jnp.float32)
    branch = reduce_rows(partial)

    input_grad = cotangents.astype(jnp.float32) + stash_scale * (
        norm_grad
        - jnp.mean(norm_grad, axis=-1, keepdims=True)
        - stash_unit * jnp.mean(norm_grad * stash_unit, axis=-1, keepdims=True)
    )
    grad_back = passed_along(input_grad.astype(jnp.bfloat16), "section", -1)

    rows_value = jnp.dot(rows_norm, weight_in, preferred_element_type=jnp.float32).astype(
        jnp.bfloat16
    )
    stash_context = mix_heads(back_probs, rows_value)
    grad_outw = jnp.einsum("th,td->hd", stash_context, rows_cot, preferred_element_type=jnp.float32)
    grad_valw = jnp.einsum("td,th->dh", rows_norm, value_back, preferred_element_type=jnp.float32)
    stash_next = lax.dynamic_update_index_in_dim(stashed, arrived, owner_slot, 0)

    layer_out = (layer_rows + branch).astype(jnp.bfloat16)
    handed_on = passed_along(layer_out, "section", 1)
    return (
        handed_on,
        grad_back,
        stash_next,
        grad_valw.astype(jnp.bfloat16)[None],
        grad_outw.astype(jnp.bfloat16)[None],
    )


def solution(mesh):
    return jax.shard_map(
        per_device,
        mesh=mesh,
        in_specs=(
            P(("section", "tp"), None),
            P(("section", "tp"), None),
            P(None, ("section", "tp"), None),
            P(),
            P("section", "tp", None, None),
            P("section", "tp", None, None),
            P("section", None, "tp"),
            P("section", "tp", None),
        ),
        out_specs=(
            P(("section", "tp"), None),
            P(("section", "tp"), None),
            P(None, ("section", "tp"), None),
            P("section", None, "tp"),
            P("section", "tp", None),
        ),
        check_vma=False,
    )
```
